32 devices in a mesh: pair: 2 (over x), seq: 4 (over z), head: 4 (over y, core).
Axes of the slice: x: 2, y: 2, z: 4, core: 2. Of those that a mesh axis runs over, the one named last changes fastest.
Arguments:
- resp_query: bfloat16 [2, 4, 256, 4096], P('pair', 'seq', None, 'head'), may hold values from -6 to 6
- resp_key: bfloat16 [2, 4, 256, 1024], P('pair', 'seq', None, 'head'), may hold values from -6 to 6
- resp_value: bfloat16 [2, 4, 256, 1024], P('pair', 'seq', None, 'head'), may hold values from -6 to 6
- direction: bfloat16 [2, 4, 256, 4096], P('pair', 'seq', None, 'head'), may hold values from -96 to 96
- ratio: float32 [2, 4, 256], P('pair', 'seq'), may hold values from -4.2 to 4.2
- lengths: int32 [2, 4], P('pair', 'seq'), may hold values from 1 to 256, 640 in all within a row
- partner: int32 [4], replicated, may hold values from 0 to 3, each once
- prompt_key: bfloat16 [1024, 1024], P('pair', 'head'), may hold values from -6 to 6
- prompt_value: bfloat16 [1024, 1024], P('pair', 'head'), may hold values from -6 to 6
Outputs:
- query_grad: bfloat16 [2, 4, 256, 4096], P('pair', 'seq', None, 'head')
- resp_key_grad: bfloat16 [2, 4, 256, 1024], P('pair', 'seq', None, 'head')
- resp_value_grad: bfloat16 [2, 4, 256, 1024], P('pair', 'seq', None, 'head')
- prompt_key_grad: bfloat16 [1024, 1024], P('pair', 'head')
- prompt_value_grad: bfloat16 [1024, 1024], P('pair', 'head')
The draws below stay inside these ranges and needn't reach their ends.
Inputs may be any that keep to these rules, and one draw needn't show every extreme that they name: On each side the response lengths sum to 640, and the longest is 256. partner names each rejected response exactly once.
All inputs are finite; a program needn't handle non-finite values. No bound on the sum of `lengths` on one device may be relied on, other than what follows from the above.
Results may differ from the reference program's by a relative error of at most 0.03.
Values may be sent and summed in bfloat16 or wider, within the bound.
A program may use at most 64 MiB of HBM per device.

```python
import math
import jax
import jax.numpy as jnp
import numpy as np
from jax import lax

KV_HEADS = 8
HEAD_DIM = 128
GROUP_WIN = 4
RESP = 256
HEADS = 32
RESPONSES = 4
PROMPT = 1024


def draw_resp_query(key, part):
    full_shape = (2, RESPONSES, RESP, KV_HEADS * GROUP_WIN * HEAD_DIM)
    drawn = jnp.clip(jax.random.normal(key, full_shape, jnp.float32), -6.0, 6.0)
    return drawn.astype(jnp.bfloat16)


def draw_prompt_key(key, part):
    full_shape = (PROMPT, KV_HEADS * HEAD_DIM)
    drawn = jnp.clip(jax.random.normal(key, full_shape, jnp.float32), -6.0, 6.0)
    return drawn.astype(jnp.bfloat16)


def draw_ratio(key, part):
    full_shape = (2, RESPONSES, RESP)
    resp_rank = jnp.arange(RESPONSES, dtype=jnp.float32)
    spread = 0.4 * (1.0 + 2.0 * resp_rank / max(RESPONSES - 1, 1))
    drawn = jnp.clip(jax.random.normal(key, full_shape, jnp.float32), -3.5, 3.5)
    return (drawn * spread[None, :, None]).astype(jnp.float32)


def block_levels(stream_key, extent, pieces, smallest, largest):
    factor_of = 1.0
    for dim, blocks in pieces:
        draws = jax.random.uniform(jax.random.fold_in(jax.random.fold_in(stream_key, 6), dim), (blocks,), jnp.float32, smallest / len(pieces), largest / len(pieces))
        factor_of = factor_of * jnp.repeat(jnp.exp(draws), extent[dim] // blocks).reshape((-1,) + (1,) * (len(extent) - 1 - dim))
    return factor_of


def length_profile(number_of, total, reach, lean):
    portions = [(1 << 20) // math.isqrt(grade ** lean) + 1 for grade in range(2, number_of + 1)]
    spare, holding = total - reach - (number_of - 1), [1] * (number_of - 1)
    while spare > 0:
        free = [i for i in range(number_of - 1) if holding[i] < reach]
        pool, left = sum([portions[i] for i in free]), spare
        for i in free:
            more = min(reach - holding[i], max(1, left * portions[i] // pool), spare)
            holding[i] = holding[i] + more
            spare = spare - more
    return np.array([reach] + holding)


def uneven(rng, amount, total, reach, slope):
    if amount == 2:
        one = jax.random.randint(rng, (), max(1, total - reach), min(reach, total - 1) + 1)
        return jnp.stack([one, total - one])
    sizes = jnp.asarray(length_profile(amount, total, reach, slope), jnp.int32)
    couples = (amount - 1) // 2
    donor, sink = sizes[1:1 + 2 * couples:2], sizes[2:2 + 2 * couples:2]
    margin = jnp.minimum(donor - 1, reach - sink)
    passed = jax.random.randint(jax.random.fold_in(rng, 1), (couples,), 0, 1 << 20) % (margin + 1)
    sizes = sizes.at[1:1 + 2 * couples:2].set(donor - passed).at[2:2 + 2 * couples:2].set(sink + passed)
    return sizes[jax.random.permutation(jax.random.fold_in(rng, 2), amount)]


def gaussian(rng, dims, scale, most, cuts=(), held_as=jnp.bfloat16):
    result = scale * jax.random.normal(rng, dims, jnp.float32)
    if cuts:
        result = result * block_levels(rng, dims, cuts, -0.22, 0.18)
    return jnp.clip(result, -most, most).astype(held_as)


def setup_inputs(seed: int = 0) -> dict:
    keys = jax.random.split(jax.random.key(seed), 10)
    resp_query = draw_resp_query(jax.random.fold_in(keys[9], 71), 0)
    resp_key = gaussian(keys[1], (2, RESPONSES, RESP, KV_HEADS * HEAD_DIM), 1.0, 6.0, ((0, 2), (1, 4), (3, 4)))
    resp_value = gaussian(keys[2], (2, RESPONSES, RESP, KV_HEADS * HEAD_DIM), 1.0, 6.0, ((0, 2), (1, 4), (3, 4)))
    direction = gaussian(keys[3], (2, RESPONSES, RESP, HEADS * HEAD_DIM), 16.0, 96.0, ((0, 2), (1, 4), (3, 4)))
    ratio = draw_ratio(jax.random.fold_in(keys[9], 71), 0)
    lengths = jax.vmap(lambda own: uneven(own, RESPONSES, 5 * RESPONSES * RESP // 8, RESP, 2))(jax.random.split(keys[5], 2)).reshape((2, RESPONSES)).astype(jnp.int32)
    partner = jax.random.permutation(keys[6], RESPONSES).astype(jnp.int32)
    prompt_key = draw_prompt_key(jax.random.fold_in(keys[9], 71), 0)
    prompt_value = gaussian(keys[8], (PROMPT, KV_HEADS * HEAD_DIM), 1.0, 6.0, ((0, 2), (1, 4)))
    return dict(resp_query=resp_query, resp_key=resp_key, resp_value=resp_value, direction=direction, ratio=ratio, lengths=lengths, partner=partner, prompt_key=prompt_key, prompt_value=prompt_value)


dpo_beta = 0.1

def attend(query_rows, resp_k, resp_v, cot_rows, length, prompt_k, prompt_v):
    resp_rows = query_rows.shape[0]
    prompt_rows = prompt_k.shape[0]
    score_scale = 1.0 / math.sqrt(HEAD_DIM)
    positions = jnp.arange(resp_rows, dtype=jnp.int32)
    causal = (positions[None, :] <= positions[:, None]) & (positions[None, :] < length)
    visible = jnp.concatenate([jnp.ones((resp_rows, prompt_rows), dtype=jnp.bool_), causal], axis=1)
    query_parts, key_parts, value_parts, prompt_key_parts, prompt_value_parts = ([], [], [], [], [])
    for kv_index in range(KV_HEADS):
        head_cols = slice(kv_index * GROUP_WIN * HEAD_DIM, (kv_index + 1) * GROUP_WIN * HEAD_DIM)
        key_cols = slice(kv_index * HEAD_DIM, (kv_index + 1) * HEAD_DIM)
        key_rows = jnp.concatenate([prompt_k[:, key_cols], resp_k[:, key_cols]], 0).astype(jnp.float32)
        value_rows = jnp.concatenate([prompt_v[:, key_cols], resp_v[:, key_cols]], 0).astype(jnp.float32)
        query_f = query_rows[:, head_cols].reshape(resp_rows, GROUP_WIN, HEAD_DIM).astype(jnp.float32)
        grad_f = cot_rows[:, head_cols].reshape(resp_rows, GROUP_WIN, HEAD_DIM).astype(jnp.float32)
        scores = jnp.einsum('sgd,kd->sgk', query_f, key_rows) * score_scale
        scores = jnp.where(visible[:, None, :], scores, -jnp.inf)
        row_max = lax.optimization_barrier(jnp.max(scores, axis=2, keepdims=True))
        exponent = jnp.exp(scores - row_max)
        attn_prob = exponent / lax.optimization_barrier(jnp.sum(exponent, axis=2, keepdims=True))
        prob_half = lax.optimization_barrier(attn_prob.astype(jnp.bfloat16)).astype(jnp.float32)
        attended = jnp.einsum('sgk,kd->sgd', prob_half, value_rows)
        attended = lax.optimization_barrier(attended.astype(jnp.bfloat16)).astype(jnp.float32)
        row_delta = lax.optimization_barrier(jnp.sum(grad_f * attended, axis=2, keepdims=True))
        prob_grad = jnp.einsum('sgd,kd->sgk', grad_f, value_rows)
        score_grad = lax.optimization_barrier((attn_prob * (prob_grad - row_delta)).astype(jnp.bfloat16)).astype(jnp.float32)
        query_out = (jnp.einsum('sgk,kd->sgd', score_grad, key_rows) * score_scale).astype(jnp.bfloat16)
        query_parts.append(query_out.reshape(resp_rows, GROUP_WIN * HEAD_DIM))
        key_term = jnp.einsum('sgk,sgd->kd', score_grad, query_f) * score_scale
        value_term = jnp.einsum('sgk,sgd->kd', prob_half, grad_f)
        prompt_key_parts.append(key_term[:prompt_rows])
        prompt_value_parts.append(value_term[:prompt_rows])
        key_parts.append(key_term[prompt_rows:].astype(jnp.bfloat16))
        value_parts.append(value_term[prompt_rows:].astype(jnp.bfloat16))
    return (jnp.concatenate(query_parts, 1), jnp.concatenate(key_parts, 1), jnp.concatenate(value_parts, 1), jnp.concatenate(prompt_key_parts, 1), jnp.concatenate(prompt_value_parts, 1))

def flatten(array):
    return array.reshape((-1,) + array.shape[2:])

def reference(resp_query, resp_key, resp_value, direction, ratio, lengths, partner, prompt_key, prompt_value):
    positions = jnp.arange(ratio.shape[2], dtype=jnp.int32)
    live_mask = positions[None, None, :] < lengths[:, :, None]
    seq_sums = lax.optimization_barrier(jnp.sum(jnp.where(live_mask, ratio, 0.0), axis=2))
    pulled = jax.nn.sigmoid(-(dpo_beta * (seq_sums[0] - seq_sums[1][partner])))
    rejected = jnp.zeros_like(pulled).at[partner].set(pulled)
    weight = jnp.stack([-pulled, rejected])
    out_grads = jnp.where(live_mask[..., None], weight[:, :, None, None] * direction.astype(jnp.float32), 0.0).astype(jnp.bfloat16)

    def per_response(totals, inputs):
        query_rows, resp_k, resp_v, cot_rows, length = inputs
        query_out, key_out, value_out, prompt_kt, prompt_vt = attend(query_rows, resp_k, resp_v, cot_rows, length, prompt_key, prompt_value)
        return ((totals[0] + prompt_kt, totals[1] + prompt_vt), (query_out, key_out, value_out))
    zeros_init = jnp.zeros(prompt_key.shape, jnp.float32)
    (prompt_kt, prompt_vt), (query_out, key_out, value_out) = lax.scan(per_response, (zeros_init, zeros_init), (flatten(resp_query), flatten(resp_key), flatten(resp_value), flatten(out_grads), lengths.reshape(-1)))
    return (query_out.reshape(resp_query.shape), key_out.reshape(resp_key.shape), value_out.reshape(resp_value.shape), prompt_kt.astype(jnp.bfloat16), prompt_vt.astype(jnp.bfloat16))
```

```python
import functools
import math

import jax
import jax.numpy as jnp
from jax import lax
from jax.experimental import pallas as pl
from jax.experimental.pallas import tpu as pltpu
from jax.sharding import PartitionSpec as P

HEAD_DIM = 128
DPO_BETA = 0.1
MESH = pl.DeviceIdType.MESH
NT = (((1,), (1,)), ((), ()))
TN = (((0,), (0,)), ((), ()))
F32 = jnp.float32
BF16 = jnp.bfloat16


def dot_nt(a, b):
    return lax.dot_general(a, b, NT, preferred_element_type=F32)


def dot_tn(a, b):
    return lax.dot_general(a, b, TN, preferred_element_type=F32)


def kernel(
    n, lengths, partner, ratio, q_in, rk_in, rv_in, dir_in, pk_in, pv_in,
    qg_out, rkg_out, rvg_out, pkg_out, pvg_out,
    table, q_rows, g_rows, pk_far, pv_far, s_buf, dp_buf, ds_buf,
    x_send, x_recv, own_acc, z_send, z_recv, z_out,
    tab_send_sem, tab_recv_sem, kv_send_sem, kv_recv_sem,
    x_send_sem, x_recv_sem, rs_send_sem, rs_recv_sem, ag_send_sem, ag_recv_sem,
):
    rows = q_in.shape[2]
    half = pk_in.shape[0]
    kv_local = rk_in.shape[3] // HEAD_DIM
    group = q_in.shape[3] // rk_in.shape[3]
    lanes = rows * group
    piece = half // n
    block = min(256, half)
    blocks = half // block
    scale = 1.0 / math.sqrt(HEAD_DIM)
    exp_scale = scale * math.log2(math.e)
    side = lax.axis_index("pair")
    seq = lax.axis_index("seq")
    head = lax.axis_index("head")
    flat = side * n + seq
    pair_dev = (1 - side, seq, head)

    def peer(offset):
        other = lax.rem(flat + offset, 2 * n)
        return (other // n, lax.rem(other, n), head)

    def seq_peer(offset):
        return lax.rem(seq + offset, n)

    barrier = pltpu.get_barrier_semaphore()
    for d in range(1, 2 * n):
        pl.semaphore_signal(barrier, inc=1, device_id=peer(d), device_id_type=MESH)
    pl.semaphore_wait(barrier, 2 * n - 1)

    kv_copies = []
    for i in range(kv_local):
        cols = pl.ds(i * HEAD_DIM, HEAD_DIM)
        for which, (src, dst) in enumerate(((pk_in, pk_far), (pv_in, pv_far))):
            slot = 2 * i + which
            copy = pltpu.make_async_remote_copy(
                src_ref=src.at[:, cols], dst_ref=dst.at[i],
                send_sem=kv_send_sem.at[slot], recv_sem=kv_recv_sem.at[slot],
                device_id=pair_dev, device_id_type=MESH,
            )
            kv_copies.append(copy)

    length = lengths[0, 0]
    position = lax.broadcasted_iota(jnp.int32, (1, rows), 1)
    own_sum = jnp.sum(jnp.where(position < length, ratio[0], 0.0), axis=1, keepdims=True)
    table[flat] = jnp.broadcast_to(own_sum, (1, HEAD_DIM))
    tab_copies = []
    for d in range(1, 2 * n):
        copy = pltpu.make_async_remote_copy(
            src_ref=table.at[flat], dst_ref=table.at[flat],
            send_sem=tab_send_sem.at[d - 1], recv_sem=tab_recv_sem.at[d - 1],
            device_id=peer(d), device_id_type=MESH,
        )
        copy.start()
        tab_copies.append(copy)
    for copy in kv_copies:
        copy.start()

    for i in range(kv_local):
        for g in range(group):
            cols = slice((i * group + g) * HEAD_DIM, (i * group + g + 1) * HEAD_DIM)
            q_rows[i, g * rows:(g + 1) * rows, :] = q_in[0, 0, :, cols]

    def build_grads():
        for copy in tab_copies:
            copy.wait_recv()
        zero = jnp.zeros((1, HEAD_DIM), F32)
        mine = partner[seq]
        chosen, rejected = table[seq], zero
        chosen_r, rejected_r = zero, table[n + seq]
        for r in range(n):
            rejected = rejected + jnp.where(mine == r, table[n + r], 0.0)
            chosen_r = chosen_r + jnp.where(partner[r] == seq, table[r], 0.0)
        gap = jnp.where(side == 0, chosen - rejected, chosen_r - rejected_r)
        pulled = 1.0 / (1.0 + jnp.exp(DPO_BETA * gap))
        weight = jnp.where(side == 0, -pulled, pulled)
        live = lax.broadcasted_iota(jnp.int32, (rows, HEAD_DIM), 0) < length
        for i in range(kv_local):
            for g in range(group):
                cols = slice((i * group + g) * HEAD_DIM, (i * group + g + 1) * HEAD_DIM)
                value = weight * dir_in[0, 0, :, cols].astype(F32)
                g_rows[i, g * rows:(g + 1) * rows, :] = jnp.where(live, value, 0.0).astype(BF16)

    far_at, own_at, resp_at = 0, half, 2 * half

    def segments(i):
        cols = slice(i * HEAD_DIM, (i + 1) * HEAD_DIM)
        own = [
            (own_at + b * block, lambda b=b: pk_in[b * block:(b + 1) * block, cols],
             lambda b=b: pv_in[b * block:(b + 1) * block, cols])
            for b in range(blocks)
        ]
        resp = [(resp_at, lambda: rk_in[0, 0, :, cols], lambda: rv_in[0, 0, :, cols])]
        far = [
            (far_at + b * block, lambda b=b: pk_far[i, b * block:(b + 1) * block, :],
             lambda b=b: pv_far[i, b * block:(b + 1) * block, :])
            for b in range(blocks)
        ]
        return own, resp, far

    def score_block(i, at, keys, top, masked):
        scores = dot_nt(keys, q_rows[i])
        if masked:
            key_pos = lax.broadcasted_iota(jnp.int32, scores.shape, 0)
            row_pos = lax.rem(lax.broadcasted_iota(jnp.int32, scores.shape, 1), rows)
            scores = jnp.where((key_pos <= row_pos) & (key_pos < length), scores, -jnp.inf)
        s_buf[at:at + scores.shape[0], :] = scores
        return jnp.maximum(top, jnp.max(scores, axis=0, keepdims=True))

    def near_scores(i):
        own, resp, _ = segments(i)
        top = jnp.full((1, lanes), -jnp.inf, F32)
        for at, key, _v in own:
            top = score_block(i, at, key(), top, False)
        for at, key, _v in resp:
            top = score_block(i, at, key(), top, True)
        return top

    def far_scores(i, top):
        kv_copies[2 * i].wait_recv()
        for at, key, _v in segments(i)[2]:
            top = score_block(i, at, key(), top, False)
        return top

    def exp_pass(i, top):
        own, resp, far = segments(i)
        shift = top * exp_scale
        total = jnp.zeros((1, lanes), F32)
        delta = jnp.zeros((1, lanes), F32)
        for at, _k, value in own + resp + far:
            if at == far_at:
                kv_copies[2 * i + 1].wait_recv()
            v = value()
            span = slice(at, at + v.shape[0])
            e = jnp.exp2(s_buf[span, :] * exp_scale - shift)
            s_buf[span, :] = e
            dp = dot_nt(v, g_rows[i])
            dp_buf[span, :] = dp
            total = total + jnp.sum(e, axis=0, keepdims=True)
            delta = delta + jnp.sum(e * dp, axis=0, keepdims=True)
        inv = 1.0 / total
        return inv, delta * inv

    def grad_block(i, at, size, inv, delta):
        span = slice(at, at + size)
        prob = s_buf[span, :] * inv
        ds = (prob * (dp_buf[span, :] - delta)).astype(BF16)
        ds_buf[i, span, :] = ds
        dk = jnp.dot(ds, q_rows[i], preferred_element_type=F32) * scale
        dv = jnp.dot(prob.astype(BF16), g_rows[i], preferred_element_type=F32)
        return dk, dv

    def x_copy(i, b):
        slot = i * blocks + b
        return pltpu.make_async_remote_copy(
            src_ref=x_send.at[slot], dst_ref=x_recv.at[slot],
            send_sem=x_send_sem.at[slot], recv_sem=x_recv_sem.at[slot],
            device_id=pair_dev, device_id_type=MESH,
        )

    def grad_pass(i, inv, delta):
        for b in range(blocks):
            dk, dv = grad_block(i, far_at + b * block, block, inv, delta)
            x_send[i * blocks + b, :, :HEAD_DIM] = dk.astype(BF16)
            x_send[i * blocks + b, :, HEAD_DIM:] = dv.astype(BF16)
            x_copy(i, b).start()
        for b in range(blocks):
            dk, dv = grad_block(i, own_at + b * block, block, inv, delta)
            own_acc[i, b * block:(b + 1) * block, :HEAD_DIM] = dk
            own_acc[i, b * block:(b + 1) * block, HEAD_DIM:] = dv

    def resp_pass(i, inv, delta):
        dk, dv = grad_block(i, resp_at, rows, inv, delta)
        cols = slice(i * HEAD_DIM, (i + 1) * HEAD_DIM)
        rkg_out[0, 0, :, cols] = dk.astype(BF16)
        rvg_out[0, 0, :, cols] = dv.astype(BF16)

    def rs_copy(i, d):
        slot = i * (n - 1) + d - 1
        return pltpu.make_async_remote_copy(
            src_ref=z_send.at[i, seq_peer(d)], dst_ref=z_recv.at[slot],
            send_sem=rs_send_sem.at[slot], recv_sem=rs_recv_sem.at[slot],
            device_id=(side, seq_peer(d), head), device_id_type=MESH,
        )

    def ag_copy(i, d):
        slot = i * (n - 1) + d - 1
        return pltpu.make_async_remote_copy(
            src_ref=z_out.at[i, seq], dst_ref=z_out.at[i, seq],
            send_sem=ag_send_sem.at[slot], recv_sem=ag_recv_sem.at[slot],
            device_id=(side, seq_peer(d), head), device_id_type=MESH,
        )

    def start_rs(i):
        for b in range(blocks):
            x_copy(i, b).wait_recv()
        for p in range(n):
            b, at = p * piece // block, p * piece % block
            both = own_acc[i, p * piece:(p + 1) * piece, :] + x_recv[
                i * blocks + b, at:at + piece, :
            ].astype(F32)
            z_send[i, p] = both.astype(BF16)
        for d in range(1, n):
            rs_copy(i, d).start()

    def start_ag(i):
        total = z_send[i, seq].astype(F32)
        for d in range(1, n):
            rs_copy(i, d).wait_recv()
            total = total + z_recv[i * (n - 1) + d - 1].astype(F32)
        z_out[i, seq] = total.astype(BF16)
        for d in range(1, n):
            ag_copy(i, d).start()

    def finish(i):
        for d in range(1, n):
            ag_copy(i, d).wait_recv()
        cols = slice(i * HEAD_DIM, (i + 1) * HEAD_DIM)
        for p in range(n):
            at = slice(p * piece, (p + 1) * piece)
            pkg_out[at, cols] = z_out[i, p, :, :HEAD_DIM]
            pvg_out[at, cols] = z_out[i, p, :, HEAD_DIM:]

    def query_pass(i):
        own, resp, far = segments(i)
        total = jnp.zeros((HEAD_DIM, lanes), F32)
        for at, key, _v in own + resp + far:
            keys = key()
            total = total + dot_tn(keys, ds_buf[i, at:at + keys.shape[0], :])
        total = total * scale
        for g in range(group):
            cols = slice((i * group + g) * HEAD_DIM, (i * group + g + 1) * HEAD_DIM)
            qg_out[0, 0, :, cols] = total[:, g * rows:(g + 1) * rows].T.astype(BF16)

    for i in range(kv_local):
        top = near_scores(i)
        if i == 0:
            build_grads()
        top = far_scores(i, top)
        if i > 0:
            start_rs(i - 1)
        inv, delta = exp_pass(i, top)
        if i > 0:
            start_ag(i - 1)
        grad_pass(i, inv, delta)
        resp_pass(i, inv, delta)
    for i in range(kv_local - 1):
        query_pass(i)
    start_rs(kv_local - 1)
    query_pass(kv_local - 1)
    start_ag(kv_local - 1)
    for i in range(kv_local):
        finish(i)
    for copy in tab_copies + kv_copies:
        copy.wait_send()
    for i in range(kv_local):
        for b in range(blocks):
            x_copy(i, b).wait_send()
        for d in range(1, n):
            rs_copy(i, d).wait_send()
            ag_copy(i, d).wait_send()


def shards(
    n, resp_query, resp_key, resp_value, direction, ratio, lengths, partner, prompt_key, prompt_value
):
    rows = resp_query.shape[2]
    half, key_width = prompt_key.shape
    kv_local = key_width // HEAD_DIM
    lanes = rows * resp_query.shape[3] // key_width
    keys = 2 * half + rows
    piece = half // n
    block = min(256, half)
    blocks = half // block
    hops = max(kv_local * (n - 1), 1)
    vmem = pl.BlockSpec(memory_space=pltpu.VMEM)
    smem = pl.BlockSpec(memory_space=pltpu.SMEM)
    dma = pltpu.SemaphoreType.DMA
    return pl.pallas_call(
        functools.partial(kernel, n),
        out_shape=(
            jax.ShapeDtypeStruct(resp_query.shape, BF16),
            jax.ShapeDtypeStruct(resp_key.shape, BF16),
            jax.ShapeDtypeStruct(resp_value.shape, BF16),
            jax.ShapeDtypeStruct(prompt_key.shape, BF16),
            jax.ShapeDtypeStruct(prompt_value.shape, BF16),
        ),
        in_specs=[smem, smem] + [vmem] * 7,
        out_specs=(vmem,) * 5,
        scratch_shapes=[
            pltpu.VMEM((2 * n, 1, HEAD_DIM), F32),
            pltpu.VMEM((kv_local, lanes, HEAD_DIM), BF16),
            pltpu.VMEM((kv_local, lanes, HEAD_DIM), BF16),
            pltpu.VMEM((kv_local, half, HEAD_DIM), BF16),
            pltpu.VMEM((kv_local, half, HEAD_DIM), BF16),
            pltpu.VMEM((keys, lanes), F32),
            pltpu.VMEM((keys, lanes), F32),
            pltpu.VMEM((kv_local, keys, lanes), BF16),
            pltpu.VMEM((kv_local * blocks, block, 2 * HEAD_DIM), BF16),
            pltpu.VMEM((kv_local * blocks, block, 2 * HEAD_DIM), BF16),
            pltpu.VMEM((kv_local, half, 2 * HEAD_DIM), F32),
            pltpu.VMEM((kv_local, n, piece, 2 * HEAD_DIM), BF16),
            pltpu.VMEM((hops, piece, 2 * HEAD_DIM), BF16),
            pltpu.VMEM((kv_local, n, piece, 2 * HEAD_DIM), BF16),
            dma((2 * n - 1,)), dma((2 * n - 1,)),
            dma((2 * kv_local,)), dma((2 * kv_local,)),
            dma((kv_local * blocks,)), dma((kv_local * blocks,)),
            dma((hops,)), dma((hops,)), dma((hops,)), dma((hops,)),
        ],
        compiler_params=pltpu.CompilerParams(
            collective_id=0, has_side_effects=True, vmem_limit_bytes=60 * 1024 * 1024
        ),
        name="shared_prompt_backward",
    )(lengths, partner, ratio, resp_query, resp_key, resp_value, direction, prompt_key, prompt_value)


def solution(mesh):
    per_response = P("pair", "seq", None, "head")
    per_prompt = P("pair", "head")
    in_specs = (
        per_response, per_response, per_response, per_response,
        P("pair", "seq", None), P("pair", "seq"), P(), per_prompt, per_prompt,
    )
    out_specs = (per_response, per_response, per_response, per_prompt, per_prompt)
    return jax.shard_map(
        functools.partial(shards, mesh.shape["seq"]),
        mesh=mesh, in_specs=in_specs, out_specs=out_specs, check_vma=False,
    )
```

```python
import functools
import math

import jax
import jax.numpy as jnp
from jax import lax
from jax.experimental import pallas as pl
from jax.experimental.pallas import tpu as pltpu
from jax.sharding import PartitionSpec as P

HEAD_DIM = 128
DPO_BETA = 0.1
BLOCK = 256
UNIT = 128
MESH = pl.DeviceIdType.MESH
NT = (((1,), (1,)), ((), ()))
TN = (((0,), (0,)), ((), ()))
F32 = jnp.float32
BF16 = jnp.bfloat16


def dot_nt(a, b):
    return lax.dot_general(a, b, NT, preferred_element_type=F32)


def dot_tn(a, b):
    return lax.dot_general(a, b, TN, preferred_element_type=F32)


def kernel(
    n, lengths, partner, ratio, q_in, rk_in, rv_in, dir_in, pk_in, pv_in,
    qg_out, rkg_out, rvg_out, pkg_out, pvg_out,
    table, q_rows, g_rows, pk_far, pv_far, s_buf, dp_buf, ds_buf,
    x_send, x_recv, own_acc, c_send, c_recv,
    tab_send_sem, tab_recv_sem, kv_send_sem, kv_recv_sem,
    x_send_sem, x_recv_sem, c_send_sem, c_recv_sem,
):
    rows = q_in.shape[2]
    half = pk_in.shape[0]
    kv_local = rk_in.shape[3] // HEAD_DIM
    group = q_in.shape[3] // rk_in.shape[3]
    lanes = rows * group
    block = min(BLOCK, half)
    blocks = half // block
    unit = min(UNIT, block)
    units = half // unit
    scale = 1.0 / math.sqrt(HEAD_DIM)
    exp_scale = scale * math.log2(math.e)
    side = lax.axis_index("pair")
    seq = lax.axis_index("seq")
    head = lax.axis_index("head")
    flat = side * n + seq
    pair_dev = (1 - side, seq, head)

    def peer(offset):
        other = lax.rem(flat + offset, 2 * n)
        return (other // n, lax.rem(other, n), head)

    def seq_peer(offset):
        return lax.rem(seq + offset, n)

    barrier = pltpu.get_barrier_semaphore()
    for d in range(1, 2 * n):
        pl.semaphore_signal(barrier, inc=1, device_id=peer(d), device_id_type=MESH)

    kv_copies = []
    for i in range(kv_local):
        cols = pl.ds(i * HEAD_DIM, HEAD_DIM)
        for which, (src, dst) in enumerate(((pk_in, pk_far), (pv_in, pv_far))):
            slot = 2 * i + which
            copy = pltpu.make_async_remote_copy(
                src_ref=src.at[:, cols], dst_ref=dst.at[i],
                send_sem=kv_send_sem.at[slot], recv_sem=kv_recv_sem.at[slot],
                device_id=pair_dev, device_id_type=MESH,
            )
            kv_copies.append(copy)

    length = lengths[0, 0]
    position = lax.broadcasted_iota(jnp.int32, (1, rows), 1)
    own_sum = jnp.sum(jnp.where(position < length, ratio[0], 0.0), axis=1, keepdims=True)
    table[flat] = jnp.broadcast_to(own_sum, (1, HEAD_DIM))
    tab_copies = []

    def build_grads():
        for copy in tab_copies:
            copy.wait_recv()
        zero = jnp.zeros((1, HEAD_DIM), F32)
        mine = partner[seq]
        chosen, rejected = table[seq], zero
        chosen_r, rejected_r = zero, table[n + seq]
        for r in range(n):
            rejected = rejected + jnp.where(mine == r, table[n + r], 0.0)
            chosen_r = chosen_r + jnp.where(partner[r] == seq, table[r], 0.0)
        gap = jnp.where(side == 0, chosen - rejected, chosen_r - rejected_r)
        pulled = 1.0 / (1.0 + jnp.exp(DPO_BETA * gap))
        weight = jnp.where(side == 0, -pulled, pulled)
        live = lax.broadcasted_iota(jnp.int32, (rows, HEAD_DIM), 0) < length
        for i in range(kv_local):
            for g in range(group):
                cols = slice((i * group + g) * HEAD_DIM, (i * group + g + 1) * HEAD_DIM)
                value = weight * dir_in[0, 0, :, cols].astype(F32)
                g_rows[i, g * rows:(g + 1) * rows, :] = jnp.where(live, value, 0.0).astype(BF16)

    far_at, own_at, resp_at = 0, half, 2 * half

    def segments(i):
        cols = slice(i * HEAD_DIM, (i + 1) * HEAD_DIM)
        own = [
            (own_at + b * block, lambda b=b: pk_in[b * block:(b + 1) * block, cols],
             lambda b=b: pv_in[b * block:(b + 1) * block, cols])
            for b in range(blocks)
        ]
        resp = [(resp_at, lambda: rk_in[0, 0, :, cols], lambda: rv_in[0, 0, :, cols])]
        far = [
            (far_at + b * block, lambda b=b: pk_far[i, b * block:(b + 1) * block, :],
             lambda b=b: pv_far[i, b * block:(b + 1) * block, :])
            for b in range(blocks)
        ]
        return own, resp, far

    def score_block(i, at, keys, top, masked):
        scores = dot_nt(keys, q_rows[i])
        if masked:
            key_pos = lax.broadcasted_iota(jnp.int32, scores.shape, 0)
            row_pos = lax.rem(lax.broadcasted_iota(jnp.int32, scores.shape, 1), rows)
            scores = jnp.where((key_pos <= row_pos) & (key_pos < length), scores, -jnp.inf)
        s_buf[i, at:at + scores.shape[0], :] = scores
        return jnp.maximum(top, jnp.max(scores, axis=0, keepdims=True))

    def near_scores(i):
        own, resp, _ = segments(i)
        top = jnp.full((1, lanes), -jnp.inf, F32)
        for at, key, _v in own:
            top = score_block(i, at, key(), top, False)
        for at, key, _v in resp:
            top = score_block(i, at, key(), top, True)
        return top

    def far_scores(i, top):
        kv_copies[2 * i].wait_recv()
        for at, key, _v in segments(i)[2]:
            top = score_block(i, at, key(), top, False)
        return top

    def prob_grad_block(i, at, v):
        dp_buf[i, at:at + v.shape[0], :] = dot_nt(v, g_rows[i])

    def near_prob_grads(i):
        own, resp, _ = segments(i)
        for at, _k, value in own + resp:
            prob_grad_block(i, at, value())

    def exp_pass(i, top):
        own, resp, far = segments(i)
        shift = top * exp_scale
        total = jnp.zeros((1, lanes), F32)
        delta = jnp.zeros((1, lanes), F32)
        for at, _k, value in own + resp + far:
            if at == far_at:
                kv_copies[2 * i + 1].wait_recv()
            span = slice(at, at + (rows if at == resp_at else block))
            if at < own_at:
                prob_grad_block(i, at, value())
            e = jnp.exp2(s_buf[i, span, :] * exp_scale - shift)
            s_buf[i, span, :] = e
            total = total + jnp.sum(e, axis=0, keepdims=True)
            delta = delta + jnp.sum(e * dp_buf[i, span, :], axis=0, keepdims=True)
        inv = 1.0 / total
        return inv, delta * inv

    def grad_block(i, at, size, inv, delta):
        span = slice(at, at + size)
        prob = s_buf[i, span, :] * inv
        ds = (prob * (dp_buf[i, span, :] - delta)).astype(BF16)
        ds_buf[i, span, :] = ds
        dk = jnp.dot(ds, q_rows[i], preferred_element_type=F32) * scale
        dv = jnp.dot(prob.astype(BF16), g_rows[i], preferred_element_type=F32)
        return dk, dv

    def x_copy(u):
        return pltpu.make_async_remote_copy(
            src_ref=x_send.at[u], dst_ref=x_recv.at[u],
            send_sem=x_send_sem.at[u], recv_sem=x_recv_sem.at[u],
            device_id=pair_dev, device_id_type=MESH,
        )

    def far_pass(i, inv, delta):
        for b in range(blocks):
            dk, dv = grad_block(i, far_at + b * block, block, inv, delta)
            for k in range(block // unit):
                u = i * units + b * (block // unit) + k
                x_send[u, :, :HEAD_DIM] = dk[k * unit:(k + 1) * unit].astype(BF16)
                x_send[u, :, HEAD_DIM:] = dv[k * unit:(k + 1) * unit].astype(BF16)
                x_copy(u).start()

    def own_pass(i, inv, delta):
        for b in range(blocks):
            dk, dv = grad_block(i, own_at + b * block, block, inv, delta)
            own_acc[i, b * block:(b + 1) * block, :HEAD_DIM] = dk
            own_acc[i, b * block:(b + 1) * block, HEAD_DIM:] = dv

    def resp_pass(i, inv, delta):
        dk, dv = grad_block(i, resp_at, rows, inv, delta)
        cols = slice(i * HEAD_DIM, (i + 1) * HEAD_DIM)
        rkg_out[0, 0, :, cols] = dk.astype(BF16)
        rvg_out[0, 0, :, cols] = dv.astype(BF16)

    def chain_copy(u, way):
        turn = (1 - way) // 2
        return pltpu.make_async_remote_copy(
            src_ref=c_send.at[2 * u + turn], dst_ref=c_recv.at[2 * u + turn],
            send_sem=c_send_sem.at[2 * u + turn], recv_sem=c_recv_sem.at[2 * u + turn],
            device_id=(side, lax.rem(seq + way + n, n), head), device_id_type=MESH,
        )

    first_way = jnp.where(2 * seq < n, 1, -1)

    def chain_step(u, i, at, way):
        has_from = (seq - way >= 0) & (seq - way < n)
        has_to = (seq + way >= 0) & (seq + way < n)
        turn = (1 - way) // 2

        @pl.when(has_from)
        def _():
            chain_copy(u, way).wait_recv()

        @pl.when(has_to & has_from)
        def _():
            passed = own_acc[i, at:at + unit, :] + c_recv[2 * u + turn].astype(F32)
            c_send[2 * u + turn] = passed.astype(BF16)

        @pl.when(has_to & jnp.logical_not(has_from))
        def _():
            c_send[2 * u + turn] = own_acc[i, at:at + unit, :].astype(BF16)

        @pl.when(has_to)
        def _():
            chain_copy(u, way).start()

    def chain(u):
        i, at = u // units, u % units * unit
        x_copy(u).wait_recv()
        own_acc[i, at:at + unit, :] += x_recv[u].astype(F32)
        chain_step(u, i, at, first_way)

    def chain_back(u):
        i, at = u // units, u % units * unit
        chain_step(u, i, at, -first_way)
        cols = slice(i * HEAD_DIM, (i + 1) * HEAD_DIM)

        for way in (1, -1):
            @pl.when((seq - way >= 0) & (seq - way < n))
            def _():
                own_acc[i, at:at + unit, :] += c_recv[2 * u + (1 - way) // 2].astype(F32)
        pkg_out[at:at + unit, cols] = own_acc[i, at:at + unit, :HEAD_DIM].astype(BF16)
        pvg_out[at:at + unit, cols] = own_acc[i, at:at + unit, HEAD_DIM:].astype(BF16)

    def query_pass(i):
        own, resp, far = segments(i)
        total = jnp.zeros((HEAD_DIM, lanes), F32)
        for at, key, _v in own + resp + far:
            keys = key()
            total = total + dot_tn(keys, ds_buf[i, at:at + keys.shape[0], :])
        total = total * scale
        for g in range(group):
            cols = slice((i * group + g) * HEAD_DIM, (i * group + g + 1) * HEAD_DIM)
            qg_out[0, 0, :, cols] = total[:, g * rows:(g + 1) * rows].T.astype(BF16)

    count = kv_local * units
    for i in range(kv_local):
        for g in range(group):
            cols = slice((i * group + g) * HEAD_DIM, (i * group + g + 1) * HEAD_DIM)
            q_rows[i, g * rows:(g + 1) * rows, :] = q_in[0, 0, :, cols]
    tops = [near_scores(0)]
    pl.semaphore_wait(barrier, 2 * n - 1)
    for d in range(1, 2 * n):
        copy = pltpu.make_async_remote_copy(
            src_ref=table.at[flat], dst_ref=table.at[flat],
            send_sem=tab_send_sem.at[d - 1], recv_sem=tab_recv_sem.at[d - 1],
            device_id=peer(d), device_id_type=MESH,
        )
        copy.start()
        tab_copies.append(copy)
    for copy in kv_copies:
        copy.start()
    tops += [near_scores(i) for i in range(1, kv_local)]
    build_grads()
    for i in range(kv_local):
        near_prob_grads(i)
    stats = []
    for i in range(kv_local):
        stats.append(exp_pass(i, far_scores(i, tops[i])))
        far_pass(i, *stats[i])
        own_pass(i, *stats[i])
        if i > 0:
            for u in range((i - 1) * units, i * units):
                chain(u)
    for i in range(kv_local):
        resp_pass(i, *stats[i])
        query_pass(i)
    for u in range((kv_local - 1) * units, count):
        chain(u)
    for u in range(count):
        chain_back(u)
    for copy in tab_copies + kv_copies:
        copy.wait_send()
    for u in range(count):
        x_copy(u).wait_send()
        for way in (1, -1):
            @pl.when((seq + way >= 0) & (seq + way < n))
            def _():
                chain_copy(u, way).wait_send()


def store_kernel(count, *refs):
    sources, targets, held = refs[:count], refs[count:2 * count], refs[2 * count:3 * count]
    in_sem, out_sem = refs[3 * count:]
    loads = [
        pltpu.make_async_copy(sources[k], held[k], in_sem.at[k]) for k in range(count)
    ]
    stores = [
        pltpu.make_async_copy(held[k], targets[k], out_sem.at[k]) for k in range(count)
    ]
    for load in loads:
        load.start()
    for load, store in zip(loads, stores):
        load.wait()
        store.start()
    for store in stores:
        store.wait()


def store_all(arrays):
    count = len(arrays)
    return pl.pallas_call(
        functools.partial(store_kernel, count),
        out_shape=tuple(jax.ShapeDtypeStruct(a.shape, a.dtype) for a in arrays),
        in_specs=[pl.BlockSpec(memory_space=pl.ANY)] * count,
        out_specs=(pl.BlockSpec(memory_space=pl.ANY),) * count,
        scratch_shapes=[pltpu.VMEM(a.shape, a.dtype) for a in arrays]
        + [pltpu.SemaphoreType.DMA((count,)), pltpu.SemaphoreType.DMA((count,))],
        name="store_results",
    )(*arrays)


def shards(
    n, resp_query, resp_key, resp_value, direction, ratio, lengths, partner, prompt_key, prompt_value
):
    rows = resp_query.shape[2]
    half, key_width = prompt_key.shape
    kv_local = key_width // HEAD_DIM
    lanes = rows * resp_query.shape[3] // key_width
    keys = 2 * half + rows
    block = min(BLOCK, half)
    blocks = half // block
    unit = min(UNIT, block)
    count = kv_local * (half // unit)
    vmem = pl.BlockSpec(memory_space=pltpu.VMEM)
    smem = pl.BlockSpec(memory_space=pltpu.SMEM)
    dma = pltpu.SemaphoreType.DMA
    results = pl.pallas_call(
        functools.partial(kernel, n),
        out_shape=(
            jax.ShapeDtypeStruct(resp_query.shape, BF16),
            jax.ShapeDtypeStruct(resp_key.shape, BF16),
            jax.ShapeDtypeStruct(resp_value.shape, BF16),
            jax.ShapeDtypeStruct(prompt_key.shape, BF16),
            jax.ShapeDtypeStruct(prompt_value.shape, BF16),
        ),
        in_specs=[smem, smem] + [vmem] * 7,
        out_specs=(vmem,) * 5,
        scratch_shapes=[
            pltpu.VMEM((2 * n, 1, HEAD_DIM), F32),
            pltpu.VMEM((kv_local, lanes, HEAD_DIM), BF16),
            pltpu.VMEM((kv_local, lanes, HEAD_DIM), BF16),
            pltpu.VMEM((kv_local, half, HEAD_DIM), BF16),
            pltpu.VMEM((kv_local, half, HEAD_DIM), BF16),
            pltpu.VMEM((kv_local, keys, lanes), F32),
            pltpu.VMEM((kv_local, keys, lanes), F32),
            pltpu.VMEM((kv_local, keys, lanes), BF16),
            pltpu.VMEM((count, unit, 2 * HEAD_DIM), BF16),
            pltpu.VMEM((count, unit, 2 * HEAD_DIM), BF16),
            pltpu.VMEM((kv_local, half, 2 * HEAD_DIM), F32),
            pltpu.VMEM((2 * count, unit, 2 * HEAD_DIM), BF16),
            pltpu.VMEM((2 * count, unit, 2 * HEAD_DIM), BF16),
            dma((2 * n - 1,)), dma((2 * n - 1,)),
            dma((2 * kv_local,)), dma((2 * kv_local,)),
            dma((count,)), dma((count,)),
            dma((2 * count,)), dma((2 * count,)),
        ],
        compiler_params=pltpu.CompilerParams(
            collective_id=0, has_side_effects=True, vmem_limit_bytes=60 * 1024 * 1024
        ),
        name="shared_prompt_backward",
    )(lengths, partner, ratio, resp_query, resp_key, resp_value, direction, prompt_key, prompt_value)
    return store_all(results)


def solution(mesh):
    per_response = P("pair", "seq", None, "head")
    per_prompt = P("pair", "head")
    in_specs = (
        per_response, per_response, per_response, per_response,
        P("pair", "seq", None), P("pair", "seq"), P(), per_prompt, per_prompt,
    )
    out_specs = (per_response, per_response, per_response, per_prompt, per_prompt)
    return jax.shard_map(
        functools.partial(shards, mesh.shape["seq"]),
        mesh=mesh, in_specs=in_specs, out_specs=out_specs, check_vma=False,
    )
```
